32 devices in a mesh: row: 2 (over y), col: 16 (over z, x, core).
Axes of the slice: x: 2, y: 2, z: 4, core: 2. Of those that a mesh axis runs over, the one named last changes fastest.
Arguments:
- active_matrix: float32 [16384, 16384], P('row', 'col'), may hold values from -6 to 6
- schur_rows: float32 [512, 16384], P('row', 'col'), may hold values from -6 to 6
- accum_first: float32 [32, 512, 512], P('row', 'col'), may hold values from -1 to 1, as said below
- accum_second: float32 [32, 512, 512], P('row', 'col'), may hold values from -1 to 1, as said below
Outputs:
- matrix_out: float32 [16384, 16384], P('row', 'col')
- schur_out: float32 [512, 16384], P('row', 'col')
The draws below stay inside these ranges and needn't reach their ends.
Inputs may be any that keep to these rules, and one draw needn't show every extreme that they name: `accum_first`: each of the 32 blocks of order 512 is an orthogonal matrix. `accum_second`: each of the 32 blocks of order 512 is an orthogonal matrix.
All inputs are finite; a program needn't handle non-finite values.
Results may differ from the reference program's by a relative error of at most 0.000098.
Values sent between devices are 32-bit elements; how exact they have to be, the bound alone decides.
No kernel may reach another device: no remote copies, remote signals or barrier semaphores. Data moves between devices by JAX's collectives and lax.ppermute only.
A program may use at most 256 MiB of HBM per device.

```python
import jax
import jax.numpy as jnp
from jax import lax

N = 16384
W = 512
K = 32
ZROWS = 512


def orthogonal_blocks(key):
    normal = jax.random.normal(key, (K, W, W), jnp.float32)
    basis, upper = jnp.linalg.qr(normal)
    signs = jnp.sign(jnp.diagonal(upper, axis1=1, axis2=2))
    signs = jnp.where(signs == 0, 1.0, signs)
    return basis * signs[:, None, :]


def draw_accum_first(key, part):
    return orthogonal_blocks(jax.random.fold_in(key, 11))


def draw_accum_second(key, part):
    return orthogonal_blocks(jax.random.fold_in(key, 23))


def block_levels(own_key, extent, cuts, least, largest):
    factor_of = 1.0
    for position, shards_of in cuts:
        steps = jax.random.uniform(jax.random.fold_in(jax.random.fold_in(own_key, 6), position), (shards_of,), jnp.float32, least / len(cuts), largest / len(cuts))
        factor_of = factor_of * jnp.repeat(jnp.exp(steps), extent[position] // shards_of).reshape((-1,) + (1,) * (len(extent) - 1 - position))
    return factor_of


def bell_draw(key, shape, scale, reach, shards=(), kind=jnp.bfloat16):
    gain = block_levels(key, shape, shards, -0.22, 0.18) if shards else 1.0
    entries = jax.random.normal(key, shape, jnp.float32) * scale * gain
    return jnp.minimum(jnp.maximum(entries, -reach), reach).astype(kind)


def setup_inputs(seed: int = 0) -> dict:
    seeds = jax.random.split(jax.random.key(seed), 5)
    return {
        "active_matrix": bell_draw(seeds[0], (N, N), 1.0, 6.0, ((0, 2), (1, 16)), jnp.float32),
        "schur_rows": bell_draw(seeds[1], (ZROWS, N), 1.0, 6.0, ((0, 2), (1, 16)), jnp.float32),
        "accum_first": draw_accum_first(jax.random.fold_in(seeds[4], 71), 0),
        "accum_second": draw_accum_second(jax.random.fold_in(seeds[4], 71), 0),
    }


def left_apply(blocks, matrix):
    shaped = matrix.reshape(K, W, matrix.shape[1])
    out = jnp.einsum('kij,kin->kjn', blocks, shaped, precision=lax.Precision.HIGHEST)
    return out.reshape(N, matrix.shape[1])

def right_apply(matrix, blocks):
    rows = matrix.shape[0]
    shaped = matrix.reshape(rows, K, W)
    out = jnp.einsum('nki,kij->nkj', shaped, blocks, precision=lax.Precision.HIGHEST)
    return out.reshape(rows, N)

def reference(active_matrix, schur_rows, accum_first, accum_second):
    first_h = right_apply(left_apply(accum_first, active_matrix), accum_first)
    first_z = right_apply(schur_rows, accum_first)
    offset = W // 2
    rolled = jnp.roll(first_h, offset, (0, 1))
    second_h = right_apply(left_apply(accum_second, rolled), accum_second)
    matrix_out = jnp.roll(second_h, -offset, (0, 1))
    rolled_z = jnp.roll(first_z, offset, 1)
    schur_out = jnp.roll(right_apply(rolled_z, accum_second), -offset, 1)
    return (matrix_out, schur_out)
```

```python
import functools

import jax
import jax.numpy as jnp
from jax import lax
from jax.experimental import pallas as pl
from jax.experimental.pallas import tpu as pltpu
from jax.sharding import PartitionSpec as P

VMEM_LIMIT = 56 * 1024 * 1024


def ring(axis, distance):
    count = lax.axis_size(axis)
    return [(i, (i + distance) % count) for i in range(count)]


def split(value):
    high = value.astype(jnp.bfloat16)
    low = (value - high.astype(jnp.float32)).astype(jnp.bfloat16)
    return high, low


def dot(left, right):
    return jnp.dot(left, right, preferred_element_type=jnp.float32)


def dot_lead(left, right):
    return lax.dot_general(
        left, right, (((0,), (0,)), ((), ())), preferred_element_type=jnp.float32
    )


def cost(rows, depth, cols, *arrays):
    return pl.CostEstimate(
        flops=6 * rows * depth * cols,
        bytes_accessed=4 * sum(arrays),
        transcendentals=0,
    )


def call(kernel, **kwargs):
    return pl.pallas_call(
        kernel,
        compiler_params=pltpu.CompilerParams(
            dimension_semantics=("arbitrary",) * len(kwargs["grid"]), vmem_limit_bytes=VMEM_LIMIT
        ),
        **kwargs,
    )


def stage_blocks(block_ref, staged):
    @pl.when(pl.program_id(0) == 0)
    def _():
        count, width, _ = block_ref.shape
        for k in range(count):
            high, low = split(block_ref[k])
            staged[k, :width] = high
            staged[k, width : 2 * width] = low
            staged[k, 2 * width :] = high


def triple_cols(value):
    high, low = split(value)
    return jnp.concatenate([high, high, low], axis=1)


def triple_rows(value):
    high, low = split(value)
    return jnp.concatenate([high, high, low], axis=0)


def first_right_kernel(x_ref, u_ref, *refs):
    staged = refs[-1]
    left_ref, right_ref = refs[0], refs[1]
    stage_blocks(u_ref, staged)
    count, width, _ = u_ref.shape
    half = width // 2
    for k in range(count):
        out = dot(triple_cols(x_ref[:, k * width : (k + 1) * width]), staged[k])
        if k == 0:
            left_ref[...] = out[:, :half]
        else:
            refs[2][:, k * width - half : k * width] = out[:, :half]
        if k == count - 1:
            right_ref[...] = out[:, half:]
        else:
            refs[2][:, k * width : k * width + half] = out[:, half:]


def first_right(matrix, blocks, start, rows, tile):
    count, width, _ = blocks.shape
    half = width // 2
    cols = matrix.shape[1]
    base = start // tile
    row_block = lambda i: (i, 0)
    shapes = [(rows, half), (rows, half)]
    specs = [pl.BlockSpec((tile, half), row_block), pl.BlockSpec((tile, half), row_block)]
    if count > 1:
        shapes.append((rows, cols - width))
        specs.append(pl.BlockSpec((tile, cols - width), row_block))
    return call(
        first_right_kernel,
        grid=(rows // tile,),
        in_specs=[
            pl.BlockSpec((tile, cols), lambda i: (base + i, 0)),
            pl.BlockSpec(blocks.shape, lambda i: (0, 0, 0)),
        ],
        out_specs=specs,
        out_shape=[jax.ShapeDtypeStruct(s, jnp.float32) for s in shapes],
        scratch_shapes=[pltpu.VMEM((count, 3 * width, width), jnp.bfloat16)],
        cost_estimate=cost(rows, width, cols, 2 * rows * cols, blocks.size),
        name="first_right",
    )(matrix, blocks)


def second_right_kernel(*refs):
    pieces, (v_ref, out_ref, staged) = refs[:-3], refs[-3:]
    stage_blocks(v_ref, staged)
    count, width, _ = v_ref.shape
    half = width // 2
    x = jnp.concatenate([piece[...] for piece in pieces], axis=1)
    for j in range(count):
        part = triple_cols(x[:, j * width : (j + 1) * width])
        if j == 0:
            out_ref[:, :half] = dot(part, staged[j][:, half:])
        elif j == count - 1:
            out_ref[:, j * width - half :] = dot(part, staged[j][:, :half])
        else:
            out_ref[:, j * width - half : j * width + half] = dot(part, staged[j])


def second_right(pieces, blocks, tile):
    count, width, _ = blocks.shape
    rows = pieces[0].shape[0]
    cols = (count - 1) * width
    return call(
        second_right_kernel,
        grid=(rows // tile,),
        in_specs=[pl.BlockSpec((tile, p.shape[1]), lambda i: (i, 0)) for p in pieces]
        + [pl.BlockSpec(blocks.shape, lambda i: (0, 0, 0))],
        out_specs=pl.BlockSpec((tile, cols), lambda i: (i, 0)),
        out_shape=jax.ShapeDtypeStruct((rows, cols), jnp.float32),
        scratch_shapes=[pltpu.VMEM((count, 3 * width, width), jnp.bfloat16)],
        cost_estimate=cost(rows, width, cols, 2 * rows * cols, blocks.size),
        name="second_right",
    )(*pieces, blocks)


def triple_lead(value):
    high, low = split(value)
    return jnp.concatenate([high, low, high], axis=0)


def finish_kernel(pieces, joined, keep_head, *refs):
    parts, refs = refs[:pieces], refs[pieces:]
    cols_ref, u_ref, v_ref, refs = refs[0], refs[1], refs[2], refs[3:]
    if joined:
        above_ref, refs = refs[0], refs[1:]
    out_ref, tail_ref, *head_refs, staged, carry = refs[len(refs) - 4 - int(keep_head) :]
    stage_blocks(cols_ref, staged)
    step = pl.program_id(0)
    count, width, _ = cols_ref.shape
    half = width // 2
    x = jnp.concatenate([part[...] for part in parts], axis=1)
    moved = []
    for j in range(count):
        part = triple_cols(x[:, j * width : (j + 1) * width])
        if j == 0:
            moved.append(dot(part, staged[j][:, half:]))
        elif j == count - 1:
            moved.append(dot(part, staged[j][:, :half]))
        else:
            moved.append(dot(part, staged[j]))
    moved = jnp.concatenate(moved, axis=1)
    turned = dot_lead(triple_lead(u_ref[0]), triple_rows(moved))
    if joined:

        @pl.when(step == 0)
        def _():
            carry[...] = above_ref[...]

    if keep_head:

        @pl.when(step == 0)
        def _():
            head_refs[0][...] = turned[:half]

    straddle = jnp.concatenate([carry[...], turned[:half]], axis=0)
    out_ref[...] = dot_lead(triple_lead(v_ref[0]), triple_rows(straddle))
    carry[...] = turned[half:]
    tail_ref[...] = turned[half:]


def finish(pieces, col_blocks, row_blocks, start, count, above, buffer, shape):
    blocks, width, _ = col_blocks.shape
    half = width // 2
    cols = shape[1]
    joined, held = above is not None, buffer is not None
    keep_head = not joined
    first = start if joined else start + 1
    row_block = lambda i: (i, 0)
    whole = pl.BlockSpec((half, cols), lambda i: (0, 0))
    in_specs = [pl.BlockSpec((width, p.shape[1]), row_block) for p in pieces]
    in_specs += [
        pl.BlockSpec(col_blocks.shape, lambda i: (0, 0, 0)),
        pl.BlockSpec((1, width, width), lambda i: (i, 0, 0)),
        pl.BlockSpec((1, width, width), lambda i: (count + i, 0, 0)),
    ]
    args = [*pieces, col_blocks, row_blocks, row_blocks]
    if joined:
        in_specs.append(whole)
        args.append(above)
    if held:
        in_specs.append(pl.BlockSpec(memory_space=pl.ANY))
        args.append(buffer)
    out_spec = pl.BlockSpec(
        (pl.Element(width), pl.Element(cols)),
        lambda i: (pl.multiple_of(jnp.maximum(start + i, first) * width - half, half), 0),
    )
    edge = jax.ShapeDtypeStruct((half, cols), jnp.float32)
    return call(
        functools.partial(finish_kernel, len(pieces), joined, keep_head),
        grid=(count,),
        in_specs=in_specs,
        out_specs=[out_spec, whole] + [whole] * keep_head,
        out_shape=[jax.ShapeDtypeStruct(shape, jnp.float32), edge] + [edge] * keep_head,
        scratch_shapes=[
            pltpu.VMEM((blocks, 3 * width, width), jnp.bfloat16),
            pltpu.VMEM((half, cols), jnp.float32),
        ],
        input_output_aliases={len(args) - 1: 0} if held else {},
        cost_estimate=cost(count * width, 3 * width, cols, 3 * count * width * cols),
        name="finish",
    )(*args)


def join_kernel(above_ref, below_ref, v_ref, held, out_ref):
    del held
    straddle = jnp.concatenate([above_ref[...], below_ref[...]], axis=0)
    out_ref[...] = dot_lead(triple_lead(v_ref[0]), triple_rows(straddle))


def join(above, below, row_blocks, place, start, buffer):
    half, cols = above.shape
    width = 2 * half
    whole = pl.BlockSpec((half, cols), lambda e: (0, 0))
    return call(
        join_kernel,
        grid=(1,),
        in_specs=[
            whole,
            whole,
            pl.BlockSpec((1, width, width), lambda e: (place, 0, 0)),
            pl.BlockSpec(memory_space=pl.ANY),
        ],
        out_specs=pl.BlockSpec(
            (pl.Element(width), pl.Element(cols)), lambda e: (start, 0)
        ),
        out_shape=jax.ShapeDtypeStruct(buffer.shape, jnp.float32),
        input_output_aliases={3: 0},
        cost_estimate=cost(width, width, cols, 4 * half * cols),
        name="join",
    )(above, below, row_blocks, buffer)


def edges_kernel(above_ref, head_ref, tail_ref, below_ref, v_first, v_last, held, out_ref):
    del held
    half = head_ref.shape[0]

    @pl.when(pl.program_id(0) == 0)
    def _():
        x = jnp.concatenate([above_ref[...], head_ref[...]], axis=0)
        out_ref[...] = dot_lead(triple_lead(v_first[0][:, half:]), triple_rows(x))

    @pl.when(pl.program_id(0) == 1)
    def _():
        x = jnp.concatenate([tail_ref[...], below_ref[...]], axis=0)
        out_ref[...] = dot_lead(triple_lead(v_last[0][:, :half]), triple_rows(x))


def edges(above, head, tail, below, first_blocks, first, last_blocks, last, buffer):
    half, cols = head.shape
    width = 2 * half
    blocks = buffer.shape[0] // half
    whole = pl.BlockSpec((half, cols), lambda e: (0, 0))
    return call(
        edges_kernel,
        grid=(2,),
        in_specs=[whole] * 4
        + [
            pl.BlockSpec((1, width, width), lambda e: (first, 0, 0)),
            pl.BlockSpec((1, width, width), lambda e: (last, 0, 0)),
            pl.BlockSpec(memory_space=pl.ANY),
        ],
        out_specs=pl.BlockSpec((half, cols), lambda e: (e * (blocks - 1), 0)),
        out_shape=jax.ShapeDtypeStruct(buffer.shape, jnp.float32),
        input_output_aliases={6: 0},
        cost_estimate=cost(2 * half, width, cols, 6 * half * cols),
        name="edges",
    )(above, head, tail, below, first_blocks, last_blocks, buffer)


def column_blocks(shard, after=None):
    row = lax.axis_index("row")
    count, part, width = shard.shape
    pairs = shard.reshape(count // 2, 2, part, width)
    mine = lax.dynamic_index_in_dim(pairs, row, 1, keepdims=False)
    other = lax.dynamic_index_in_dim(pairs, 1 - row, 1, keepdims=False)
    got = lax.ppermute(other, "row", ring("row", 1))
    both = jnp.where(
        row == 0, jnp.concatenate([mine, got], axis=0), jnp.concatenate([got, mine], axis=0)
    )
    if after is not None:
        both, _ = lax.optimization_barrier((both, after))
    owned = lax.all_to_all(both, "col", 0, 1, tiled=True)[0]
    swapped = lax.ppermute(owned, "row", ring("row", 1))
    low = jnp.where(row == 0, owned, swapped)
    high = jnp.where(row == 0, swapped, owned)
    return jnp.stack([low, high]), owned


def spread_blocks(full, per_col):
    per_row = full.shape[0]
    place = lax.axis_index("col") * per_col
    chosen = lax.dynamic_slice_in_dim(full, place % per_row, per_col, 0)
    mine = lax.axis_index("row") == place // per_row
    return lax.psum(jnp.where(mine, chosen, jnp.zeros_like(chosen)), "row")


def gather(shard):
    return lax.all_gather(shard, "col", axis=1, tiled=True)


def per_device(active_matrix, schur_rows, accum_first, accum_second):
    width = accum_first.shape[2]
    row_tile, col_tile = active_matrix.shape
    per_row = row_tile // width
    per_col = col_tile // width
    rows, cols = lax.axis_size("row"), lax.axis_size("col")

    fast = rows == 2 and per_col == 2 and per_row == cols
    if fast:
        first_cols, owned = column_blocks(accum_first)
        second_cols, owned = column_blocks(accum_second, owned)
        low = lax.ppermute(
            owned, ("row", "col"), [((c + 1) % cols, c) for c in range(cols)]
        )
        high = lax.ppermute(
            owned, ("row", "col"), [((c + 1) % cols, cols + c) for c in range(cols)]
        )
        beyond = (low + high)[None]
        first_cols, _ = lax.optimization_barrier((first_cols, owned))

    following = lax.ppermute(accum_second[0:1], "row", ring("row", -1))
    cuts = [per_row * k // 16 for k in ((0, 5, 10, 12, 16) if per_row >= 16 else (0, 8, 16))]
    spans = list(zip(cuts, cuts[1:]))
    spans = spans[-1:] + spans[:-1]
    gathered = {}
    for a, b in spans:
        shards = [accum_first[a:b], accum_second[a:b]] + [following] * (b == per_row)
        gathered[a] = gather(jnp.concatenate(shards, axis=0))

    if not fast:
        order = sorted(spans)
        first_cols = spread_blocks(
            jnp.concatenate([gathered[a][: b - a] for a, b in order], axis=0), per_col
        )
        second_cols = spread_blocks(
            jnp.concatenate([gathered[a][b - a : 2 * (b - a)] for a, b in order], axis=0), per_col
        )
        beyond = lax.ppermute(second_cols[0:1], "col", ring("col", -1))
    border_cols = jnp.concatenate([second_cols, beyond], axis=0)

    def right_pieces(matrix, start, size, tile):
        left, right, *inner = first_right(matrix, first_cols, start, size, tile)
        before = lax.ppermute(right, "col", ring("col", 1))
        after = lax.ppermute(left, "col", ring("col", -1))
        return [before, left, *inner, right, after]

    pieces = {
        a: right_pieces(active_matrix, a * width, (b - a) * width, width) for a, b in spans
    }
    side = right_pieces(schur_rows, 0, schur_rows.shape[0], schur_rows.shape[0])

    last, lowest = spans[0][0], spans[1][0]
    out, above, heads, tails = None, None, {}, {}
    for k, (a, b) in enumerate(spans):
        if k == len(spans) - 1 and k > 1:
            out = close_edges(heads, tails, out)
        out, tails[a], *head = finish(
            pieces[a], border_cols, gathered[a], a, b - a, above, out, active_matrix.shape
        )
        if head:
            heads[a] = head[0]
        above = None if k == 0 else tails[a]
        if k == 1:
            from_above = lax.ppermute(tails[last], "row", ring("row", 1))
            from_below = lax.ppermute(heads[lowest], "row", ring("row", -1))
            *side, above = lax.optimization_barrier((*side, above))
            schur_out = second_right(side, border_cols, schur_rows.shape[0])
            close_edges = lambda heads, tails, out: edges(
                from_above,
                heads[lowest],
                tails[last],
                from_below,
                gathered[lowest],
                spans[1][1] - lowest,
                gathered[last],
                2 * (per_row - last),
                out,
            )
    if len(spans) == 2:
        out = close_edges(heads, tails, out)
    matrix_out = join(
        above, heads[last], gathered[last], per_row - last, last * width - width // 2, out
    )
    return (matrix_out, schur_out)


def solution(mesh):
    in_specs = (P("row", "col"), P("row", "col"), P("row", "col", None), P("row", "col", None))
    out_specs = (P("row", "col"), P("row", "col"))
    return jax.shard_map(
        per_device, mesh=mesh, in_specs=in_specs, out_specs=out_specs, check_vma=False
    )
```

```python
import functools
import math

import jax
import jax.numpy as jnp
from jax import lax
from jax.experimental import pallas as pl
from jax.experimental.pallas import tpu as pltpu
from jax.sharding import Mesh, PartitionSpec as P

VMEM_LIMIT = 56 * 1024 * 1024


COL = ("line", "side", "core")


def size_of(axis):
    if isinstance(axis, tuple):
        return math.prod(lax.axis_size(name) for name in axis)
    return lax.axis_size(axis)


def ring(axis, distance):
    count = size_of(axis)
    return [(i, (i + distance) % count) for i in range(count)]


def split(value):
    high = value.astype(jnp.bfloat16)
    low = (value - high.astype(jnp.float32)).astype(jnp.bfloat16)
    return high, low


def dot(left, right):
    return jnp.dot(left, right, preferred_element_type=jnp.float32)


def dot_lead(left, right):
    return lax.dot_general(
        left, right, (((0,), (0,)), ((), ())), preferred_element_type=jnp.float32
    )


def cost(rows, depth, cols, *arrays):
    return pl.CostEstimate(
        flops=6 * rows * depth * cols,
        bytes_accessed=4 * sum(arrays),
        transcendentals=0,
    )


def call(kernel, **kwargs):
    return pl.pallas_call(
        kernel,
        compiler_params=pltpu.CompilerParams(
            dimension_semantics=("arbitrary",) * len(kwargs["grid"]), vmem_limit_bytes=VMEM_LIMIT
        ),
        **kwargs,
    )


def stage_blocks(block_ref, staged):
    @pl.when(pl.program_id(0) == 0)
    def _():
        count, width, _ = block_ref.shape
        for k in range(count):
            high, low = split(block_ref[k])
            staged[k, :width] = high
            staged[k, width : 2 * width] = low
            staged[k, 2 * width :] = high


def triple_cols(value):
    high, low = split(value)
    return jnp.concatenate([high, high, low], axis=1)


def triple_rows(value):
    high, low = split(value)
    return jnp.concatenate([high, high, low], axis=0)


def first_right_kernel(x_ref, u_ref, *refs):
    staged = refs[-1]
    left_ref, right_ref = refs[0], refs[1]
    stage_blocks(u_ref, staged)
    count, width, _ = u_ref.shape
    half = width // 2
    for k in range(count):
        out = dot(triple_cols(x_ref[:, k * width : (k + 1) * width]), staged[k])
        if k == 0:
            left_ref[...] = out[:, :half]
        else:
            refs[2][:, k * width - half : k * width] = out[:, :half]
        if k == count - 1:
            right_ref[...] = out[:, half:]
        else:
            refs[2][:, k * width : k * width + half] = out[:, half:]


def first_right(matrix, blocks, start, rows, tile):
    count, width, _ = blocks.shape
    half = width // 2
    cols = matrix.shape[1]
    base = start // tile
    row_block = lambda i: (i, 0)
    shapes = [(rows, half), (rows, half)]
    specs = [pl.BlockSpec((tile, half), row_block), pl.BlockSpec((tile, half), row_block)]
    if count > 1:
        shapes.append((rows, cols - width))
        specs.append(pl.BlockSpec((tile, cols - width), row_block))
    return call(
        first_right_kernel,
        grid=(rows // tile,),
        in_specs=[
            pl.BlockSpec((tile, cols), lambda i: (base + i, 0)),
            pl.BlockSpec(blocks.shape, lambda i: (0, 0, 0)),
        ],
        out_specs=specs,
        out_shape=[jax.ShapeDtypeStruct(s, jnp.float32) for s in shapes],
        scratch_shapes=[pltpu.VMEM((count, 3 * width, width), jnp.bfloat16)],
        cost_estimate=cost(rows, width, cols, 2 * rows * cols, blocks.size),
        name="first_right",
    )(matrix, blocks)


def second_right_kernel(*refs):
    pieces, (v_ref, out_ref, staged) = refs[:-3], refs[-3:]
    stage_blocks(v_ref, staged)
    count, width, _ = v_ref.shape
    half = width // 2
    x = jnp.concatenate([piece[...] for piece in pieces], axis=1)
    for j in range(count + 1):
        part = triple_cols(x[:, j * width : (j + 1) * width])
        if j == 0:
            out_ref[:, :half] = dot(part, staged[0][:, :half])
        elif j == count:
            out_ref[:, j * width - half :] = dot(part, staged[0][:, half:])
        else:
            out_ref[:, j * width - half : j * width + half] = dot(part, staged[j])


def second_right(pieces, blocks, tile):
    count, width, _ = blocks.shape
    rows = pieces[0].shape[0]
    cols = count * width
    return call(
        second_right_kernel,
        grid=(rows // tile,),
        in_specs=[pl.BlockSpec((tile, p.shape[1]), lambda i: (i, 0)) for p in pieces]
        + [pl.BlockSpec(blocks.shape, lambda i: (0, 0, 0))],
        out_specs=pl.BlockSpec((tile, cols), lambda i: (i, 0)),
        out_shape=jax.ShapeDtypeStruct((rows, cols), jnp.float32),
        scratch_shapes=[pltpu.VMEM((count, 3 * width, width), jnp.bfloat16)],
        cost_estimate=cost(rows, width, cols, 2 * rows * cols, blocks.size),
        name="second_right",
    )(*pieces, blocks)


def triple_lead(value):
    high, low = split(value)
    return jnp.concatenate([high, low, high], axis=0)


def finish_kernel(joined, held, x_ref, u_ref, v_ref, *refs):
    step = pl.program_id(0)
    half = x_ref.shape[0] // 2
    out_ref, tail_ref, *head_refs, carry = refs[joined + held :]
    turned = dot_lead(triple_lead(block_of(u_ref)), triple_rows(x_ref[...]))

    @pl.when(step == 0)
    def _():
        if joined:
            carry[...] = refs[0][...]
        else:
            head_refs[0][...] = turned[:half]

    straddle = jnp.concatenate([carry[...], turned[:half]], axis=0)
    out_ref[...] = dot_lead(triple_lead(block_of(v_ref)), triple_rows(straddle))
    carry[...] = turned[half:]
    tail_ref[...] = turned[half:]


def finish(chunk, row_blocks, place, border_place, start, count, above, buffer, total):
    width = row_blocks.shape[-1]
    half = width // 2
    cols = chunk.shape[1]
    joined, held = above is not None, buffer is not None
    first = start if joined else start + 1
    whole = pl.BlockSpec((half, cols), lambda i: (0, 0))
    in_specs = [
        pl.BlockSpec((width, cols), lambda i: (i, 0)),
        block_spec(row_blocks, lambda i: place + i),
        block_spec(row_blocks, lambda i: border_place + i),
    ]
    args = [chunk, row_blocks, row_blocks]
    if joined:
        in_specs.append(whole)
        args.append(above)
    if held:
        in_specs.append(pl.BlockSpec(memory_space=pl.ANY))
        args.append(buffer)
    out_spec = pl.BlockSpec(
        (pl.Element(width), pl.Element(cols)),
        lambda i: (pl.multiple_of(jnp.maximum(start + i, first) * width - half, half), 0),
    )
    edge = jax.ShapeDtypeStruct((half, cols), jnp.float32)
    edge_count = 1 if joined else 2
    return call(
        functools.partial(finish_kernel, int(joined), int(held)),
        grid=(count,),
        in_specs=in_specs,
        out_specs=[out_spec] + [whole] * edge_count,
        out_shape=[jax.ShapeDtypeStruct((total, cols), jnp.float32)] + [edge] * edge_count,
        scratch_shapes=[pltpu.VMEM((half, cols), jnp.float32)],
        input_output_aliases={len(args) - 1: 0} if held else {},
        cost_estimate=cost(count * width, 2 * width, cols, 2 * count * width * cols),
        name="finish",
    )(*args)


def join_kernel(above_ref, below_ref, v_ref, held, out_ref):
    del held
    straddle = jnp.concatenate([above_ref[...], below_ref[...]], axis=0)
    out_ref[...] = dot_lead(triple_lead(block_of(v_ref)), triple_rows(straddle))


def join(above, below, row_blocks, place, start, buffer):
    half, cols = above.shape
    width = 2 * half
    whole = pl.BlockSpec((half, cols), lambda e: (0, 0))
    return call(
        join_kernel,
        grid=(1,),
        in_specs=[
            whole,
            whole,
            block_spec(row_blocks, lambda e: place),
            pl.BlockSpec(memory_space=pl.ANY),
        ],
        out_specs=pl.BlockSpec(
            (pl.Element(width), pl.Element(cols)), lambda e: (start, 0)
        ),
        out_shape=jax.ShapeDtypeStruct(buffer.shape, jnp.float32),
        input_output_aliases={3: 0},
        cost_estimate=cost(width, width, cols, 4 * half * cols),
        name="join",
    )(above, below, row_blocks, buffer)


def edges_kernel(above_ref, head_ref, tail_ref, below_ref, v_first, v_last, held, out_ref):
    del held
    half = head_ref.shape[0]

    @pl.when(pl.program_id(0) == 0)
    def _():
        x = jnp.concatenate([above_ref[...], head_ref[...]], axis=0)
        out_ref[...] = dot_lead(triple_lead(block_of(v_first)[:, half:]), triple_rows(x))

    @pl.when(pl.program_id(0) == 1)
    def _():
        x = jnp.concatenate([tail_ref[...], below_ref[...]], axis=0)
        out_ref[...] = dot_lead(triple_lead(block_of(v_last)[:, :half]), triple_rows(x))


def edges(above, head, tail, below, first_blocks, first, last_blocks, last, buffer):
    half, cols = head.shape
    width = 2 * half
    blocks = buffer.shape[0] // half
    whole = pl.BlockSpec((half, cols), lambda e: (0, 0))
    return call(
        edges_kernel,
        grid=(2,),
        in_specs=[whole] * 4
        + [
            block_spec(first_blocks, lambda e: first),
            block_spec(last_blocks, lambda e: last),
            pl.BlockSpec(memory_space=pl.ANY),
        ],
        out_specs=pl.BlockSpec((half, cols), lambda e: (e * (blocks - 1), 0)),
        out_shape=jax.ShapeDtypeStruct(buffer.shape, jnp.float32),
        input_output_aliases={6: 0},
        cost_estimate=cost(2 * half, width, cols, 6 * half * cols),
        name="edges",
    )(above, head, tail, below, first_blocks, last_blocks, buffer)


def column_blocks(shard, border, after=None):
    row = lax.axis_index("row")
    count, part, width = shard.shape
    half = width // 2
    pairs = shard.reshape(count // 2, 2, part, width)
    mine = lax.dynamic_index_in_dim(pairs, row, 1, keepdims=False)
    other = lax.dynamic_index_in_dim(pairs, 1 - row, 1, keepdims=False)
    got = lax.ppermute(other, "row", ring("row", 1))
    both = jnp.where(
        row == 0, jnp.concatenate([mine, got], axis=0), jnp.concatenate([got, mine], axis=0)
    )
    if border:
        shifted = jnp.concatenate([both[1:, :, :half], both[:1, :, :half]], axis=0)
        even = jnp.concatenate([both[:, :, half:], shifted], axis=2)
        both = jnp.where(row == 0, even, both)
    if after is not None:
        both, _ = lax.optimization_barrier((both, after))
    owned = lax.all_to_all(both, COL, 0, 1, tiled=True)[0]
    swapped = lax.ppermute(owned, "row", ring("row", 1))
    low = jnp.where(row == 0, owned, swapped)
    high = jnp.where(row == 0, swapped, owned)
    return jnp.stack([low, high]), owned


def spread_blocks(full, per_col):
    per_row = full.shape[0]
    place = lax.axis_index(COL) * per_col
    chosen = lax.dynamic_slice_in_dim(full, place % per_row, per_col, 0)
    mine = lax.axis_index("row") == place // per_row
    return lax.psum(jnp.where(mine, chosen, jnp.zeros_like(chosen)), "row")


def gather(shard):
    return lax.all_gather(shard, COL, axis=1, tiled=True)


def gather_line(shard, after):
    swapped = lax.ppermute(shard, "side", ring("side", 1))
    swapped, _ = lax.optimization_barrier((swapped, after))
    mine = lax.axis_index("side") == 0
    pair = jnp.stack([jnp.where(mine, shard, swapped), jnp.where(mine, swapped, shard)])
    whole = lax.all_gather(pair[None], ("line", "core"), axis=0, tiled=True)
    return whole.reshape(lax.axis_size("line"), lax.axis_size("core"), *pair.shape)


def block_spec(blocks, place):
    if blocks.ndim == 3:
        return pl.BlockSpec((1, *blocks.shape[1:]), lambda i: (place(i), 0, 0))
    line, core, side, _, part, width = blocks.shape
    return pl.BlockSpec(
        (line, core, side, 1, part, width), lambda i: (0, 0, 0, place(i), 0, 0)
    )


def block_of(ref):
    if len(ref.shape) == 3:
        return ref[0]
    line, core, side = ref.shape[:3]
    slices = [
        ref[z, c, x, 0] for z in range(line) for x in range(side) for c in range(core)
    ]
    return jnp.concatenate(slices, axis=0)


def per_device(active_matrix, schur_rows, accum_first, accum_second):
    width = accum_first.shape[2]
    row_tile, col_tile = active_matrix.shape
    per_row = row_tile // width
    per_col = col_tile // width
    rows, cols = size_of("row"), size_of(COL)

    fast = rows == 2 and per_col == 2 and per_row == cols
    if fast:
        first_cols, started = column_blocks(accum_first, False)
        border_cols, owned = column_blocks(accum_second, True, started)
        first_cols, _ = lax.optimization_barrier((first_cols, owned))

    following = lax.ppermute(accum_second[0:1], "row", ring("row", -1))
    cuts = [per_row * k // 16 for k in ((0, 7, 12, 16) if per_row >= 16 else (0, 8, 16))]
    groups = list(zip(cuts, cuts[1:]))
    groups = groups[-1:] + groups[:-1]
    gathered = {}
    for a, b in groups:
        shards = [accum_first[a:b], accum_second[a:b]] + [following] * (b == per_row)
        shard = jnp.concatenate(shards, axis=0)
        if fast and a == 0 and size_of("side") == 2:
            gathered[a, b] = gather_line(shard, started)
        else:
            gathered[a, b] = gather(shard)
    spans = [(12, 16), (0, 7), (7, 10), (10, 12)] if per_row >= 16 else [(8, 16), (0, 8)]
    spans = [(per_row * a // 16, per_row * b // 16) for a, b in spans]

    def row_blocks(window):
        a, b = next(g for g in groups if g[0] <= window < g[1])
        return gathered[a, b], window - a, b - a + window - a

    if not fast:
        order = sorted(groups)
        first_cols = spread_blocks(
            jnp.concatenate([gathered[a, b][: b - a] for a, b in order], axis=0), per_col
        )
        second_cols = spread_blocks(
            jnp.concatenate([gathered[a, b][b - a : 2 * (b - a)] for a, b in order], axis=0),
            per_col,
        )
        beyond = lax.ppermute(second_cols[0:1], COL, ring(COL, -1))
        half = width // 2
        ends = jnp.concatenate([second_cols[:1, :, half:], beyond[:, :, :half]], axis=2)
        border_cols = jnp.concatenate([ends, second_cols[1:]], axis=0)

    def right_pieces(matrix, blocks, start, size, tile):
        left, right, *inner = first_right(matrix, blocks, start, size, tile)
        before = lax.ppermute(right, COL, ring(COL, 1))
        after = lax.ppermute(left, COL, ring(COL, -1))
        return [before, left, *inner, right, after]

    side = right_pieces(schur_rows, first_cols, 0, schur_rows.shape[0], schur_rows.shape[0])
    blocks, _ = lax.optimization_barrier((first_cols, side[1]))
    pieces = {}
    for a, b in spans:
        pieces[a] = right_pieces(active_matrix, blocks, a * width, (b - a) * width, width)
        blocks, _ = lax.optimization_barrier((first_cols, pieces[a][1]))
    border_cols, _ = lax.optimization_barrier((border_cols, blocks))
    last, lowest = spans[0][0], spans[1][0]
    out, above, heads, tails = None, None, {}, {}
    for k, (a, b) in enumerate(spans):
        if k == 2:
            out = close_edges(out)
        chunk = second_right(pieces[a], border_cols, width)
        out, tails[a], *head = finish(
            chunk, *row_blocks(a), a, b - a, above, out, row_tile
        )
        if head:
            heads[a] = head[0]
        if k == 0:
            border_cols, _ = lax.optimization_barrier((border_cols, tails[a]))
        above = None if k == 0 else tails[a]
        if k == 1:
            *side, above = lax.optimization_barrier((*side, above))
            schur_out = second_right(side, border_cols, schur_rows.shape[0])
        if k == 1:
            from_above = lax.ppermute(tails[last], "row", ring("row", 1))
            from_below = lax.ppermute(heads[lowest], "row", ring("row", -1))
            held_first, _, first_place = row_blocks(lowest)
            held_last, _, last_place = row_blocks(per_row - 1)
            close_edges = lambda out: edges(
                from_above,
                heads[lowest],
                tails[last],
                from_below,
                held_first,
                first_place,
                held_last,
                last_place + 1,
                out,
            )
    if len(spans) == 2:
        out = close_edges(out)
    held_join, _, join_place = row_blocks(last)
    matrix_out = join(above, heads[last], held_join, join_place, last * width - width // 2, out)
    return (matrix_out, schur_out)


def solution(mesh):
    rows, cols = mesh.devices.shape
    core = 2 if cols % 2 == 0 else 1
    chips = cols // core
    side = 1
    while chips % (2 * side) == 0 and 4 * side * side <= chips:
        side *= 2
    fine = Mesh(mesh.devices.reshape(rows, chips // side, side, core), ("row", *COL))
    in_specs = (P("row", COL), P("row", COL), P("row", COL, None), P("row", COL, None))
    out_specs = (P("row", COL), P("row", COL))
    return jax.shard_map(
        per_device, mesh=fine, in_specs=in_specs, out_specs=out_specs, check_vma=False
    )
```

```python
import functools
import math

import jax
import jax.numpy as jnp
from jax import lax
from jax.experimental import pallas as pl
from jax.experimental.pallas import tpu as pltpu
from jax.sharding import Mesh, PartitionSpec as P

VMEM_LIMIT = 56 * 1024 * 1024


COL = ("line", "side", "core")


def size_of(axis):
    if isinstance(axis, tuple):
        return math.prod(lax.axis_size(name) for name in axis)
    return lax.axis_size(axis)


def ring(axis, distance):
    count = size_of(axis)
    return [(i, (i + distance) % count) for i in range(count)]


def split(value):
    high = value.astype(jnp.bfloat16)
    low = (value - high.astype(jnp.float32)).astype(jnp.bfloat16)
    return high, low


def dot(left, right):
    return jnp.dot(left, right, preferred_element_type=jnp.float32)


def dot_lead(left, right):
    return lax.dot_general(
        left, right, (((0,), (0,)), ((), ())), preferred_element_type=jnp.float32
    )


def cost(rows, depth, cols, *arrays):
    return pl.CostEstimate(
        flops=6 * rows * depth * cols,
        bytes_accessed=4 * sum(arrays),
        transcendentals=0,
    )


def call(kernel, **kwargs):
    return pl.pallas_call(
        kernel,
        compiler_params=pltpu.CompilerParams(
            dimension_semantics=("arbitrary",) * len(kwargs["grid"]), vmem_limit_bytes=VMEM_LIMIT
        ),
        **kwargs,
    )


def stage_blocks(block_ref, staged):
    @pl.when(pl.program_id(0) == 0)
    def _():
        count, width, _ = block_ref.shape
        for k in range(count):
            high, low = split(block_ref[k])
            staged[k, :width] = high
            staged[k, width : 2 * width] = low
            staged[k, 2 * width :] = high


def triple_cols(value):
    high, low = split(value)
    return jnp.concatenate([high, high, low], axis=1)


def triple_rows(value):
    high, low = split(value)
    return jnp.concatenate([high, high, low], axis=0)


def first_right_kernel(x_ref, u_ref, *refs):
    staged = refs[-1]
    left_ref, right_ref = refs[0], refs[1]
    stage_blocks(u_ref, staged)
    count, width, _ = u_ref.shape
    half = width // 2
    for k in range(count):
        out = dot(triple_cols(x_ref[:, k * width : (k + 1) * width]), staged[k])
        if k == 0:
            left_ref[...] = out[:, :half]
        else:
            refs[2][:, k * width - half : k * width] = out[:, :half]
        if k == count - 1:
            right_ref[...] = out[:, half:]
        else:
            refs[2][:, k * width : k * width + half] = out[:, half:]


def first_right(matrix, blocks, start, rows, tile):
    count, width, _ = blocks.shape
    half = width // 2
    cols = matrix.shape[1]
    base = start // tile
    row_block = lambda i: (i, 0)
    shapes = [(rows, half), (rows, half)]
    specs = [pl.BlockSpec((tile, half), row_block), pl.BlockSpec((tile, half), row_block)]
    if count > 1:
        shapes.append((rows, cols - width))
        specs.append(pl.BlockSpec((tile, cols - width), row_block))
    return call(
        first_right_kernel,
        grid=(rows // tile,),
        in_specs=[
            pl.BlockSpec((tile, cols), lambda i: (base + i, 0)),
            pl.BlockSpec(blocks.shape, lambda i: (0, 0, 0)),
        ],
        out_specs=specs,
        out_shape=[jax.ShapeDtypeStruct(s, jnp.float32) for s in shapes],
        scratch_shapes=[pltpu.VMEM((count, 3 * width, width), jnp.bfloat16)],
        cost_estimate=cost(rows, width, cols, 2 * rows * cols, blocks.size),
        name="first_right",
    )(matrix, blocks)


def second_right_kernel(*refs):
    pieces, (v_ref, out_ref, staged) = refs[:-3], refs[-3:]
    stage_blocks(v_ref, staged)
    count, width, _ = v_ref.shape
    half = width // 2
    x = jnp.concatenate([piece[...] for piece in pieces], axis=1)
    for j in range(count + 1):
        part = triple_cols(x[:, j * width : (j + 1) * width])
        if j == 0:
            out_ref[:, :half] = dot(part, staged[0][:, :half])
        elif j == count:
            out_ref[:, j * width - half :] = dot(part, staged[0][:, half:])
        else:
            out_ref[:, j * width - half : j * width + half] = dot(part, staged[j])


def second_right(pieces, blocks, tile):
    count, width, _ = blocks.shape
    rows = pieces[0].shape[0]
    cols = count * width
    return call(
        second_right_kernel,
        grid=(rows // tile,),
        in_specs=[pl.BlockSpec((tile, p.shape[1]), lambda i: (i, 0)) for p in pieces]
        + [pl.BlockSpec(blocks.shape, lambda i: (0, 0, 0))],
        out_specs=pl.BlockSpec((tile, cols), lambda i: (i, 0)),
        out_shape=jax.ShapeDtypeStruct((rows, cols), jnp.float32),
        scratch_shapes=[pltpu.VMEM((count, 3 * width, width), jnp.bfloat16)],
        cost_estimate=cost(rows, width, cols, 2 * rows * cols, blocks.size),
        name="second_right",
    )(*pieces, blocks)


def triple_lead(value):
    high, low = split(value)
    return jnp.concatenate([high, low, high], axis=0)


def finish_kernel(joined, held, x_ref, u_ref, v_ref, *refs):
    step = pl.program_id(0)
    half = x_ref.shape[0] // 2
    out_ref, tail_ref, *head_refs, carry = refs[joined + held :]
    turned = dot_lead(triple_lead(block_of(u_ref)), triple_rows(x_ref[...]))

    @pl.when(step == 0)
    def _():
        if joined:
            carry[...] = refs[0][...]
        else:
            head_refs[0][...] = turned[:half]

    straddle = jnp.concatenate([carry[...], turned[:half]], axis=0)
    out_ref[...] = dot_lead(triple_lead(block_of(v_ref)), triple_rows(straddle))
    carry[...] = turned[half:]
    tail_ref[...] = turned[half:]


def finish(chunk, row_blocks, place, border_place, start, count, above, buffer, total):
    width = row_blocks.shape[-1]
    half = width // 2
    cols = chunk.shape[1]
    joined, held = above is not None, buffer is not None
    first = start if joined else start + 1
    whole = pl.BlockSpec((half, cols), lambda i: (0, 0))
    in_specs = [
        pl.BlockSpec((width, cols), lambda i: (i, 0)),
        block_spec(row_blocks, lambda i: place + i),
        block_spec(row_blocks, lambda i: border_place + i),
    ]
    args = [chunk, row_blocks, row_blocks]
    if joined:
        in_specs.append(whole)
        args.append(above)
    if held:
        in_specs.append(pl.BlockSpec(memory_space=pl.ANY))
        args.append(buffer)
    out_spec = pl.BlockSpec(
        (pl.Element(width), pl.Element(cols)),
        lambda i: (pl.multiple_of(jnp.maximum(start + i, first) * width - half, half), 0),
    )
    edge = jax.ShapeDtypeStruct((half, cols), jnp.float32)
    edge_count = 1 if joined else 2
    return call(
        functools.partial(finish_kernel, int(joined), int(held)),
        grid=(count,),
        in_specs=in_specs,
        out_specs=[out_spec] + [whole] * edge_count,
        out_shape=[jax.ShapeDtypeStruct((total, cols), jnp.float32)] + [edge] * edge_count,
        scratch_shapes=[pltpu.VMEM((half, cols), jnp.float32)],
        input_output_aliases={len(args) - 1: 0} if held else {},
        cost_estimate=cost(count * width, 2 * width, cols, 2 * count * width * cols),
        name="finish",
    )(*args)


def join_kernel(above_ref, below_ref, v_ref, held, out_ref):
    del held
    straddle = jnp.concatenate([above_ref[...], below_ref[...]], axis=0)
    out_ref[...] = dot_lead(triple_lead(block_of(v_ref)), triple_rows(straddle))


def join(above, below, row_blocks, place, start, buffer):
    half, cols = above.shape
    width = 2 * half
    whole = pl.BlockSpec((half, cols), lambda e: (0, 0))
    return call(
        join_kernel,
        grid=(1,),
        in_specs=[
            whole,
            whole,
            block_spec(row_blocks, lambda e: place),
            pl.BlockSpec(memory_space=pl.ANY),
        ],
        out_specs=pl.BlockSpec(
            (pl.Element(width), pl.Element(cols)), lambda e: (start, 0)
        ),
        out_shape=jax.ShapeDtypeStruct(buffer.shape, jnp.float32),
        input_output_aliases={3: 0},
        cost_estimate=cost(width, width, cols, 4 * half * cols),
        name="join",
    )(above, below, row_blocks, buffer)


def edges_kernel(above_ref, head_ref, tail_ref, below_ref, v_first, v_last, held, out_ref):
    del held
    half = head_ref.shape[0]

    @pl.when(pl.program_id(0) == 0)
    def _():
        x = jnp.concatenate([above_ref[...], head_ref[...]], axis=0)
        out_ref[...] = dot_lead(triple_lead(block_of(v_first)[:, half:]), triple_rows(x))

    @pl.when(pl.program_id(0) == 1)
    def _():
        x = jnp.concatenate([tail_ref[...], below_ref[...]], axis=0)
        out_ref[...] = dot_lead(triple_lead(block_of(v_last)[:, :half]), triple_rows(x))


def edges(above, head, tail, below, first_blocks, first, last_blocks, last, buffer):
    half, cols = head.shape
    width = 2 * half
    blocks = buffer.shape[0] // half
    whole = pl.BlockSpec((half, cols), lambda e: (0, 0))
    return call(
        edges_kernel,
        grid=(2,),
        in_specs=[whole] * 4
        + [
            block_spec(first_blocks, lambda e: first),
            block_spec(last_blocks, lambda e: last),
            pl.BlockSpec(memory_space=pl.ANY),
        ],
        out_specs=pl.BlockSpec((half, cols), lambda e: (e * (blocks - 1), 0)),
        out_shape=jax.ShapeDtypeStruct(buffer.shape, jnp.float32),
        input_output_aliases={6: 0},
        cost_estimate=cost(2 * half, width, cols, 6 * half * cols),
        name="edges",
    )(above, head, tail, below, first_blocks, last_blocks, buffer)


def column_blocks(shard, border, after=None):
    row = lax.axis_index("row")
    count, part, width = shard.shape
    half = width // 2
    pairs = shard.reshape(count // 2, 2, part, width)
    mine = lax.dynamic_index_in_dim(pairs, row, 1, keepdims=False)
    other = lax.dynamic_index_in_dim(pairs, 1 - row, 1, keepdims=False)
    got = lax.ppermute(other, "row", ring("row", 1))
    both = jnp.where(
        row == 0, jnp.concatenate([mine, got], axis=0), jnp.concatenate([got, mine], axis=0)
    )
    if border:
        shifted = jnp.concatenate([both[1:, :, :half], both[:1, :, :half]], axis=0)
        even = jnp.concatenate([both[:, :, half:], shifted], axis=2)
        both = jnp.where(row == 0, even, both)
    if after is not None:
        both, _ = lax.optimization_barrier((both, after))
    owned = lax.all_to_all(both, COL, 0, 1, tiled=True)[0]
    swapped = lax.ppermute(owned, "row", ring("row", 1))
    low = jnp.where(row == 0, owned, swapped)
    high = jnp.where(row == 0, swapped, owned)
    return jnp.stack([low, high]), owned, got


def spread_blocks(full, per_col):
    per_row = full.shape[0]
    place = lax.axis_index(COL) * per_col
    chosen = lax.dynamic_slice_in_dim(full, place % per_row, per_col, 0)
    mine = lax.axis_index("row") == place // per_row
    return lax.psum(jnp.where(mine, chosen, jnp.zeros_like(chosen)), "row")


def gather(shard):
    return lax.all_gather(shard, COL, axis=1, tiled=True)


def gather_line(shard, before, after):
    shard, _ = lax.optimization_barrier((shard, before))
    swapped = lax.ppermute(shard, "side", ring("side", 1))
    swapped, _ = lax.optimization_barrier((swapped, after))
    mine = lax.axis_index("side") == 0
    pair = jnp.stack([jnp.where(mine, shard, swapped), jnp.where(mine, swapped, shard)])
    whole = lax.all_gather(pair[None], ("line", "core"), axis=0, tiled=True)
    return whole.reshape(lax.axis_size("line"), lax.axis_size("core"), *pair.shape)


def block_spec(blocks, place):
    if blocks.ndim == 3:
        return pl.BlockSpec((1, *blocks.shape[1:]), lambda i: (place(i), 0, 0))
    line, core, side, _, part, width = blocks.shape
    return pl.BlockSpec(
        (line, core, side, 1, part, width), lambda i: (0, 0, 0, place(i), 0, 0)
    )


def block_of(ref):
    if len(ref.shape) == 3:
        return ref[0]
    line, core, side = ref.shape[:3]
    slices = [
        ref[z, c, x, 0] for z in range(line) for x in range(side) for c in range(core)
    ]
    return jnp.concatenate(slices, axis=0)


def per_device(active_matrix, schur_rows, accum_first, accum_second):
    width = accum_first.shape[2]
    row_tile, col_tile = active_matrix.shape
    per_row = row_tile // width
    per_col = col_tile // width
    rows, cols = size_of("row"), size_of(COL)

    fast = rows == 2 and per_col == 2 and per_row == cols
    if fast:
        first_cols, started, _ = column_blocks(accum_first, False)
        border_cols, owned, met = column_blocks(accum_second, True, started)
        first_cols, _ = lax.optimization_barrier((first_cols, owned))

    following = lax.ppermute(accum_second[0:1], "row", ring("row", -1))
    cuts = [per_row * k // 16 for k in ((0, 7, 12, 16) if per_row >= 16 else (0, 8, 16))]
    groups = list(zip(cuts, cuts[1:]))
    groups = groups[-1:] + groups[:-1]
    gathered = {}
    for a, b in groups:
        shards = [accum_first[a:b], accum_second[a:b]] + [following] * (b == per_row)
        shard = jnp.concatenate(shards, axis=0)
        if fast and a == 0 and size_of("side") == 2:
            gathered[a, b] = gather_line(shard, met, started)
        else:
            gathered[a, b] = gather(shard)
    spans = [(12, 16), (0, 7), (7, 10), (10, 12)] if per_row >= 16 else [(8, 16), (0, 8)]
    spans = [(per_row * a // 16, per_row * b // 16) for a, b in spans]

    def row_blocks(window):
        a, b = next(g for g in groups if g[0] <= window < g[1])
        return gathered[a, b], window - a, b - a + window - a

    if not fast:
        order = sorted(groups)
        first_cols = spread_blocks(
            jnp.concatenate([gathered[a, b][: b - a] for a, b in order], axis=0), per_col
        )
        second_cols = spread_blocks(
            jnp.concatenate([gathered[a, b][b - a : 2 * (b - a)] for a, b in order], axis=0),
            per_col,
        )
        beyond = lax.ppermute(second_cols[0:1], COL, ring(COL, -1))
        half = width // 2
        ends = jnp.concatenate([second_cols[:1, :, half:], beyond[:, :, :half]], axis=2)
        border_cols = jnp.concatenate([ends, second_cols[1:]], axis=0)

    def right_pieces(matrix, blocks, start, size, tile):
        left, right, *inner = first_right(matrix, blocks, start, size, tile)
        before = lax.ppermute(right, COL, ring(COL, 1))
        after = lax.ppermute(left, COL, ring(COL, -1))
        return [before, left, *inner, right, after]

    side = right_pieces(schur_rows, first_cols, 0, schur_rows.shape[0], schur_rows.shape[0])
    blocks, _ = lax.optimization_barrier((first_cols, side[1]))
    pieces = {}
    for a, b in spans:
        pieces[a] = right_pieces(active_matrix, blocks, a * width, (b - a) * width, width)
        blocks, _ = lax.optimization_barrier((first_cols, pieces[a][1]))
    border_cols, _ = lax.optimization_barrier((border_cols, blocks))
    last, lowest = spans[0][0], spans[1][0]
    out, above, heads, tails = None, None, {}, {}
    for k, (a, b) in enumerate(spans):
        if k == 2:
            out = close_edges(out)
        chunk = second_right(pieces[a], border_cols, width)
        out, tails[a], *head = finish(
            chunk, *row_blocks(a), a, b - a, above, out, row_tile
        )
        if head:
            heads[a] = head[0]
        if k == 0:
            border_cols, _ = lax.optimization_barrier((border_cols, tails[a]))
        above = None if k == 0 else tails[a]
        if k == 1:
            *side, above = lax.optimization_barrier((*side, above))
            schur_out = second_right(side, border_cols, schur_rows.shape[0])
        if k == 1:
            from_above = lax.ppermute(tails[last], "row", ring("row", 1))
            from_below = lax.ppermute(heads[lowest], "row", ring("row", -1))
            held_first, _, first_place = row_blocks(lowest)
            held_last, _, last_place = row_blocks(per_row - 1)
            close_edges = lambda out: edges(
                from_above,
                heads[lowest],
                tails[last],
                from_below,
                held_first,
                first_place,
                held_last,
                last_place + 1,
                out,
            )
    if len(spans) == 2:
        out = close_edges(out)
    held_join, _, join_place = row_blocks(last)
    matrix_out = join(above, heads[last], held_join, join_place, last * width - width // 2, out)
    return (matrix_out, schur_out)


def solution(mesh):
    rows, cols = mesh.devices.shape
    core = 2 if cols % 2 == 0 else 1
    chips = cols // core
    side = 1
    while chips % (2 * side) == 0 and 4 * side * side <= chips:
        side *= 2
    fine = Mesh(mesh.devices.reshape(rows, chips // side, side, core), ("row", *COL))
    in_specs = (P("row", COL), P("row", COL), P("row", COL, None), P("row", COL, None))
    out_specs = (P("row", COL), P("row", COL))
    return jax.shard_map(
        per_device, mesh=fine, in_specs=in_specs, out_specs=out_specs, check_vma=False
    )
```

```python
import functools
import math

import jax
import jax.numpy as jnp
from jax import lax
from jax.experimental import pallas as pl
from jax.experimental.pallas import tpu as pltpu
from jax.sharding import Mesh, PartitionSpec as P

VMEM_LIMIT = 56 * 1024 * 1024


COL = ("line", "side", "core")


def size_of(axis):
    if isinstance(axis, tuple):
        return math.prod(lax.axis_size(name) for name in axis)
    return lax.axis_size(axis)


def ring(axis, distance):
    count = size_of(axis)
    return [(i, (i + distance) % count) for i in range(count)]


def split(value):
    high = value.astype(jnp.bfloat16)
    low = (value - high.astype(jnp.float32)).astype(jnp.bfloat16)
    return high, low


def dot(left, right):
    return jnp.dot(left, right, preferred_element_type=jnp.float32)


def dot_lead(left, right):
    return lax.dot_general(
        left, right, (((0,), (0,)), ((), ())), preferred_element_type=jnp.float32
    )


def cost(rows, depth, cols, *arrays):
    return pl.CostEstimate(
        flops=6 * rows * depth * cols,
        bytes_accessed=4 * sum(arrays),
        transcendentals=0,
    )


def call(kernel, **kwargs):
    return pl.pallas_call(
        kernel,
        compiler_params=pltpu.CompilerParams(
            dimension_semantics=("arbitrary",) * len(kwargs["grid"]), vmem_limit_bytes=VMEM_LIMIT
        ),
        **kwargs,
    )


def stage_blocks(block_ref, staged):
    @pl.when(pl.program_id(0) == 0)
    def _():
        count, width, _ = block_ref.shape
        for k in range(count):
            high, low = split(block_ref[k])
            staged[k, :width] = high
            staged[k, width : 2 * width] = low
            staged[k, 2 * width :] = high


def triple_cols(value):
    high, low = split(value)
    return jnp.concatenate([high, high, low], axis=1)


def triple_rows(value):
    high, low = split(value)
    return jnp.concatenate([high, high, low], axis=0)


def first_right_kernel(x_ref, u_ref, *refs):
    staged = refs[-1]
    left_ref, right_ref = refs[0], refs[1]
    stage_blocks(u_ref, staged)
    count, width, _ = u_ref.shape
    half = width // 2
    for k in range(count):
        out = dot(triple_cols(x_ref[:, k * width : (k + 1) * width]), staged[k])
        if k == 0:
            left_ref[...] = out[:, :half]
        else:
            refs[2][:, k * width - half : k * width] = out[:, :half]
        if k == count - 1:
            right_ref[...] = out[:, half:]
        else:
            refs[2][:, k * width : k * width + half] = out[:, half:]


def first_right(matrix, blocks, start, rows, tile):
    count, width, _ = blocks.shape
    half = width // 2
    cols = matrix.shape[1]
    base = start // tile
    row_block = lambda i: (i, 0)
    shapes = [(rows, half), (rows, half)]
    specs = [pl.BlockSpec((tile, half), row_block), pl.BlockSpec((tile, half), row_block)]
    if count > 1:
        shapes.append((rows, cols - width))
        specs.append(pl.BlockSpec((tile, cols - width), row_block))
    return call(
        first_right_kernel,
        grid=(rows // tile,),
        in_specs=[
            pl.BlockSpec((tile, cols), lambda i: (base + i, 0)),
            pl.BlockSpec(blocks.shape, lambda i: (0, 0, 0)),
        ],
        out_specs=specs,
        out_shape=[jax.ShapeDtypeStruct(s, jnp.float32) for s in shapes],
        scratch_shapes=[pltpu.VMEM((count, 3 * width, width), jnp.bfloat16)],
        cost_estimate=cost(rows, width, cols, 2 * rows * cols, blocks.size),
        name="first_right",
    )(matrix, blocks)


def second_right_kernel(*refs):
    pieces, (v_ref, out_ref, staged) = refs[:-3], refs[-3:]
    stage_blocks(v_ref, staged)
    count, width, _ = v_ref.shape
    half = width // 2
    x = jnp.concatenate([piece[...] for piece in pieces], axis=1)
    for j in range(count + 1):
        part = triple_cols(x[:, j * width : (j + 1) * width])
        if j == 0:
            out_ref[:, :half] = dot(part, staged[0][:, :half])
        elif j == count:
            out_ref[:, j * width - half :] = dot(part, staged[0][:, half:])
        else:
            out_ref[:, j * width - half : j * width + half] = dot(part, staged[j])


def second_right(pieces, blocks, tile):
    count, width, _ = blocks.shape
    rows = pieces[0].shape[0]
    cols = count * width
    return call(
        second_right_kernel,
        grid=(rows // tile,),
        in_specs=[pl.BlockSpec((tile, p.shape[1]), lambda i: (i, 0)) for p in pieces]
        + [pl.BlockSpec(blocks.shape, lambda i: (0, 0, 0))],
        out_specs=pl.BlockSpec((tile, cols), lambda i: (i, 0)),
        out_shape=jax.ShapeDtypeStruct((rows, cols), jnp.float32),
        scratch_shapes=[pltpu.VMEM((count, 3 * width, width), jnp.bfloat16)],
        cost_estimate=cost(rows, width, cols, 2 * rows * cols, blocks.size),
        name="second_right",
    )(*pieces, blocks)


def triple_lead(value):
    high, low = split(value)
    return jnp.concatenate([high, low, high], axis=0)


def finish_kernel(joined, held, x_ref, u_ref, v_ref, *refs):
    step = pl.program_id(0)
    half = x_ref.shape[0] // 2
    out_ref, tail_ref, *head_refs, carry = refs[joined + held :]
    turned = dot_lead(triple_lead(block_of(u_ref)), triple_rows(x_ref[...]))

    @pl.when(step == 0)
    def _():
        if joined:
            carry[...] = refs[0][...]
        else:
            head_refs[0][...] = turned[:half]

    straddle = jnp.concatenate([carry[...], turned[:half]], axis=0)
    out_ref[...] = dot_lead(triple_lead(block_of(v_ref)), triple_rows(straddle))
    carry[...] = turned[half:]
    tail_ref[...] = turned[half:]


def finish(chunk, row_blocks, place, border_place, start, count, above, buffer, total):
    width = row_blocks.shape[-1]
    half = width // 2
    cols = chunk.shape[1]
    joined, held = above is not None, buffer is not None
    first = start if joined else start + 1
    whole = pl.BlockSpec((half, cols), lambda i: (0, 0))
    in_specs = [
        pl.BlockSpec((width, cols), lambda i: (i, 0)),
        block_spec(row_blocks, lambda i: place + i),
        block_spec(row_blocks, lambda i: border_place + i),
    ]
    args = [chunk, row_blocks, row_blocks]
    if joined:
        in_specs.append(whole)
        args.append(above)
    if held:
        in_specs.append(pl.BlockSpec(memory_space=pl.ANY))
        args.append(buffer)
    out_spec = pl.BlockSpec(
        (pl.Element(width), pl.Element(cols)),
        lambda i: (pl.multiple_of(jnp.maximum(start + i, first) * width - half, half), 0),
    )
    edge = jax.ShapeDtypeStruct((half, cols), jnp.float32)
    edge_count = 1 if joined else 2
    return call(
        functools.partial(finish_kernel, int(joined), int(held)),
        grid=(count,),
        in_specs=in_specs,
        out_specs=[out_spec] + [whole] * edge_count,
        out_shape=[jax.ShapeDtypeStruct((total, cols), jnp.float32)] + [edge] * edge_count,
        scratch_shapes=[pltpu.VMEM((half, cols), jnp.float32)],
        input_output_aliases={len(args) - 1: 0} if held else {},
        cost_estimate=cost(count * width, 2 * width, cols, 2 * count * width * cols),
        name="finish",
    )(*args)


def join_kernel(above_ref, below_ref, v_ref, held, out_ref):
    del held
    straddle = jnp.concatenate([above_ref[...], below_ref[...]], axis=0)
    out_ref[...] = dot_lead(triple_lead(block_of(v_ref)), triple_rows(straddle))


def join(above, below, row_blocks, place, start, buffer):
    half, cols = above.shape
    width = 2 * half
    whole = pl.BlockSpec((half, cols), lambda e: (0, 0))
    return call(
        join_kernel,
        grid=(1,),
        in_specs=[
            whole,
            whole,
            block_spec(row_blocks, lambda e: place),
            pl.BlockSpec(memory_space=pl.ANY),
        ],
        out_specs=pl.BlockSpec(
            (pl.Element(width), pl.Element(cols)), lambda e: (start, 0)
        ),
        out_shape=jax.ShapeDtypeStruct(buffer.shape, jnp.float32),
        input_output_aliases={3: 0},
        cost_estimate=cost(width, width, cols, 4 * half * cols),
        name="join",
    )(above, below, row_blocks, buffer)


def edges_kernel(above_ref, head_ref, tail_ref, below_ref, v_first, v_last, held, out_ref):
    del held
    half = head_ref.shape[0]

    @pl.when(pl.program_id(0) == 0)
    def _():
        x = jnp.concatenate([above_ref[...], head_ref[...]], axis=0)
        out_ref[...] = dot_lead(triple_lead(block_of(v_first)[:, half:]), triple_rows(x))

    @pl.when(pl.program_id(0) == 1)
    def _():
        x = jnp.concatenate([tail_ref[...], below_ref[...]], axis=0)
        out_ref[...] = dot_lead(triple_lead(block_of(v_last)[:, :half]), triple_rows(x))


def edges(above, head, tail, below, first_blocks, first, last_blocks, last, buffer):
    half, cols = head.shape
    width = 2 * half
    blocks = buffer.shape[0] // half
    whole = pl.BlockSpec((half, cols), lambda e: (0, 0))
    return call(
        edges_kernel,
        grid=(2,),
        in_specs=[whole] * 4
        + [
            block_spec(first_blocks, lambda e: first),
            block_spec(last_blocks, lambda e: last),
            pl.BlockSpec(memory_space=pl.ANY),
        ],
        out_specs=pl.BlockSpec((half, cols), lambda e: (e * (blocks - 1), 0)),
        out_shape=jax.ShapeDtypeStruct(buffer.shape, jnp.float32),
        input_output_aliases={6: 0},
        cost_estimate=cost(2 * half, width, cols, 6 * half * cols),
        name="edges",
    )(above, head, tail, below, first_blocks, last_blocks, buffer)


def column_blocks(shard, border, after=None):
    row = lax.axis_index("row")
    count, part, width = shard.shape
    half = width // 2
    pairs = shard.reshape(count // 2, 2, part, width)
    mine = lax.dynamic_index_in_dim(pairs, row, 1, keepdims=False)
    other = lax.dynamic_index_in_dim(pairs, 1 - row, 1, keepdims=False)
    got = lax.ppermute(other, "row", ring("row", 1))
    both = jnp.where(
        row == 0, jnp.concatenate([mine, got], axis=0), jnp.concatenate([got, mine], axis=0)
    )
    if border:
        shifted = jnp.concatenate([both[1:, :, :half], both[:1, :, :half]], axis=0)
        even = jnp.concatenate([both[:, :, half:], shifted], axis=2)
        both = jnp.where(row == 0, even, both)
    if after is not None:
        both, _ = lax.optimization_barrier((both, after))
    owned = lax.all_to_all(both, COL, 0, 1, tiled=True)[0]
    swapped = lax.ppermute(owned, "row", ring("row", 1))
    low = jnp.where(row == 0, owned, swapped)
    high = jnp.where(row == 0, swapped, owned)
    return jnp.stack([low, high]), owned


def spread_blocks(full, per_col):
    per_row = full.shape[0]
    place = lax.axis_index(COL) * per_col
    chosen = lax.dynamic_slice_in_dim(full, place % per_row, per_col, 0)
    mine = lax.axis_index("row") == place // per_row
    return lax.psum(jnp.where(mine, chosen, jnp.zeros_like(chosen)), "row")


def gather(shard):
    return lax.all_gather(shard, COL, axis=1, tiled=True)


def gather_line(shard, after):
    swapped = lax.ppermute(shard, "side", ring("side", 1))
    swapped, _ = lax.optimization_barrier((swapped, after))
    mine = lax.axis_index("side") == 0
    pair = jnp.stack([jnp.where(mine, shard, swapped), jnp.where(mine, swapped, shard)])
    whole = lax.all_gather(pair[None], ("line", "core"), axis=0, tiled=True)
    return whole.reshape(lax.axis_size("line"), lax.axis_size("core"), *pair.shape)


def block_spec(blocks, place):
    if blocks.ndim == 3:
        return pl.BlockSpec((1, *blocks.shape[1:]), lambda i: (place(i), 0, 0))
    line, core, side, _, part, width = blocks.shape
    return pl.BlockSpec(
        (line, core, side, 1, part, width), lambda i: (0, 0, 0, place(i), 0, 0)
    )


def block_of(ref):
    if len(ref.shape) == 3:
        return ref[0]
    line, core, side = ref.shape[:3]
    slices = [
        ref[z, c, x, 0] for z in range(line) for x in range(side) for c in range(core)
    ]
    return jnp.concatenate(slices, axis=0)


def per_device(active_matrix, schur_rows, accum_first, accum_second):
    width = accum_first.shape[2]
    row_tile, col_tile = active_matrix.shape
    per_row = row_tile // width
    per_col = col_tile // width
    rows, cols = size_of("row"), size_of(COL)

    fast = rows == 2 and per_col == 2 and per_row == cols
    if fast:
        first_cols, started = column_blocks(accum_first, False)
        border_cols, owned = column_blocks(accum_second, True, started)
        first_cols, _ = lax.optimization_barrier((first_cols, owned))

    following = lax.ppermute(accum_second[0:1], "row", ring("row", -1))
    cuts = [per_row * k // 16 for k in ((0, 8, 12, 16) if per_row >= 16 else (0, 8, 16))]
    groups = list(zip(cuts, cuts[1:]))
    groups = groups[-1:] + groups[:-1]
    gathered = {}
    for a, b in groups:
        shards = [accum_first[a:b], accum_second[a:b]] + [following] * (b == per_row)
        shard = jnp.concatenate(shards, axis=0)
        if fast and a == 0 and size_of("side") == 2:
            gathered[a, b] = gather_line(shard, started)
        else:
            gathered[a, b] = gather(shard)
    spans = [(12, 16), (0, 8), (8, 10), (10, 12)] if per_row >= 16 else [(8, 16), (0, 8)]
    spans = [(per_row * a // 16, per_row * b // 16) for a, b in spans]

    def row_blocks(window):
        a, b = next(g for g in groups if g[0] <= window < g[1])
        return gathered[a, b], window - a, b - a + window - a

    if not fast:
        order = sorted(groups)
        first_cols = spread_blocks(
            jnp.concatenate([gathered[a, b][: b - a] for a, b in order], axis=0), per_col
        )
        second_cols = spread_blocks(
            jnp.concatenate([gathered[a, b][b - a : 2 * (b - a)] for a, b in order], axis=0),
            per_col,
        )
        beyond = lax.ppermute(second_cols[0:1], COL, ring(COL, -1))
        half = width // 2
        ends = jnp.concatenate([second_cols[:1, :, half:], beyond[:, :, :half]], axis=2)
        border_cols = jnp.concatenate([ends, second_cols[1:]], axis=0)

    def right_pieces(matrix, blocks, start, size, tile):
        left, right, *inner = first_right(matrix, blocks, start, size, tile)
        before = lax.ppermute(right, COL, ring(COL, 1))
        after = lax.ppermute(left, COL, ring(COL, -1))
        return [before, left, *inner, right, after]

    side = right_pieces(schur_rows, first_cols, 0, schur_rows.shape[0], schur_rows.shape[0])
    blocks, _ = lax.optimization_barrier((first_cols, side[1]))
    pieces = {}
    for a, b in spans:
        pieces[a] = right_pieces(active_matrix, blocks, a * width, (b - a) * width, width)
        blocks, _ = lax.optimization_barrier((first_cols, pieces[a][1]))
    border_cols, _ = lax.optimization_barrier((border_cols, blocks))
    last, lowest = spans[0][0], spans[1][0]
    out, above, heads, tails = None, None, {}, {}
    for k, (a, b) in enumerate(spans):
        if k == 2:
            out = close_edges(out)
        chunk = second_right(pieces[a], border_cols, width)
        out, tails[a], *head = finish(
            chunk, *row_blocks(a), a, b - a, above, out, row_tile
        )
        if head:
            heads[a] = head[0]
        if k == 0:
            border_cols, _ = lax.optimization_barrier((border_cols, tails[a]))
        above = None if k == 0 else tails[a]
        if k == 1:
            *side, above = lax.optimization_barrier((*side, above))
            schur_out = second_right(side, border_cols, schur_rows.shape[0])
        if k == 1:
            from_above = lax.ppermute(tails[last], "row", ring("row", 1))
            from_below = lax.ppermute(heads[lowest], "row", ring("row", -1))
            held_first, _, first_place = row_blocks(lowest)
            held_last, _, last_place = row_blocks(per_row - 1)
            close_edges = lambda out: edges(
                from_above,
                heads[lowest],
                tails[last],
                from_below,
                held_first,
                first_place,
                held_last,
                last_place + 1,
                out,
            )
    if len(spans) == 2:
        out = close_edges(out)
    held_join, _, join_place = row_blocks(last)
    matrix_out = join(above, heads[last], held_join, join_place, last * width - width // 2, out)
    return (matrix_out, schur_out)


def solution(mesh):
    rows, cols = mesh.devices.shape
    core = 2 if cols % 2 == 0 else 1
    chips = cols // core
    side = 1
    while chips % (2 * side) == 0 and 4 * side * side <= chips:
        side *= 2
    fine = Mesh(mesh.devices.reshape(rows, chips // side, side, core), ("row", *COL))
    in_specs = (P("row", COL), P("row", COL), P("row", COL, None), P("row", COL, None))
    out_specs = (P("row", COL), P("row", COL))
    return jax.shard_map(
        per_device, mesh=fine, in_specs=in_specs, out_specs=out_specs, check_vma=False
    )
```
